32 devices in a mesh: bas: 8 (over y, x, core), aux: 4 (over z).
Axes of the slice: x: 2, y: 2, z: 4, core: 2. Of those that a mesh axis runs over, the one named last changes fastest.
Arguments:
- integrals: bfloat16 [4, 8192, 8192], P('aux', 'bas'), may hold values from -6 to 6
- screen: int32 [4, 64, 64], P('aux', 'bas'), may hold values from 0 to 1, as said below
- coefficients: bfloat16 [8192, 384], P('bas'), may hold values from -0.0625 to 0.0625
- weights: float32 [384], replicated, may hold values from -2 to 2
Outputs:
- exchange: bfloat16 [8192, 8192], P('aux', 'bas')
The draws below stay inside these ranges and needn't reach their ends.
Inputs may be any that keep to these rules, and one draw needn't show every extreme that they name: `screen`: every block with equal row and column block index is 1; the share of ones differs from row block to row block.
All inputs are finite; a program needn't handle non-finite values.
Results may differ from the reference program's by a relative error of at most 0.018.
Values may be sent and summed in bfloat16 or wider, within the bound.
A program may use at most 128 MiB of HBM per device.

```python
import math
import jax
import jax.numpy as jnp
from jax import lax

NBF = 8192
NOCC = 384
BLOCK = 128
AUX_DEV = 1
NAUX = 4
NB = 64
N_AUX = 4


def draw_screen(key, part):
    first_key, second_key = jax.random.split(jax.random.fold_in(key, 17))
    levels = jax.random.randint(first_key, (1, NB, 1), 15, 96)
    values = jax.random.randint(second_key, (NAUX, NB, NB), 0, 100)
    kept = (values < levels).astype(jnp.int32)
    diagonal = jnp.eye(NB, dtype=jnp.int32)[None, :, :]
    return jnp.maximum(kept, diagonal)


def block_scale(own_key, extent, cuts, least, top_value):
    def one(position, blocks):
        heights = jax.random.uniform(jax.random.fold_in(jax.random.fold_in(own_key, 6), position), (blocks,), jnp.float32, least / len(cuts), top_value / len(cuts))
        return jnp.repeat(jnp.exp(heights), extent[position] // blocks).reshape((-1,) + (1,) * (len(extent) - position - 1))

    level = one(*cuts[0])
    for cut in cuts[1:]:
        level = level * one(*cut)
    return level


def centred(stream_key, shape, width, reach, pieces=(), kind=jnp.bfloat16):
    values = jax.random.normal(stream_key, shape, jnp.float32) * width
    if len(pieces) > 0:
        values = block_scale(stream_key, shape, pieces, -0.22, 0.18) * values
    return jnp.clip(values, min=-reach, max=reach).astype(kind)


def setup_inputs(seed: int = 0) -> dict:
    splits = jax.random.split(jax.random.key(seed), 5)
    integrals = centred(splits[0], (NAUX, NBF, NBF), 1.0, 6.0, ((0, 4), (1, 8)))
    screen = draw_screen(jax.random.fold_in(splits[4], 71), 0)
    coefficients = centred(splits[2], (NBF, NOCC), NBF ** -0.5, 0.0625, ((0, 8),))
    weights = jnp.clip(jax.random.uniform(splits[3], (NOCC,), jnp.float32, -2.0, 2.0), -2.0, 2.0)
    return {"integrals": integrals, "screen": screen, "coefficients": coefficients, "weights": weights}


def reference(integrals, screen, coefficients, weights):
    nblk = NBF // BLOCK
    blocks = integrals.reshape(N_AUX, AUX_DEV, nblk, BLOCK, nblk, BLOCK)
    masks = screen.reshape(N_AUX, AUX_DEV, nblk, 1, nblk, 1).astype(jnp.bfloat16)
    tiled = jnp.tile(weights, AUX_DEV)
    factor = coefficients.astype(jnp.float32)

    def accumulate(total, pair):
        block, mask = pair
        masked = (block * mask).reshape(AUX_DEV, NBF, NBF)
        half = jnp.einsum('pml,li->mpi', masked.astype(jnp.float32), factor)
        half = half.reshape(NBF, AUX_DEV * NOCC).astype(jnp.bfloat16)
        weighted = (half.astype(jnp.float32) * tiled).astype(jnp.bfloat16)
        term = lax.dot_general(half, weighted, (((1,), (1,)), ((), ())), preferred_element_type=jnp.float32)
        rounded = lax.optimization_barrier(term.astype(jnp.bfloat16))
        return (total + rounded.astype(jnp.float32), None)
    start_total = jnp.zeros((NBF, NBF), jnp.float32)
    total, _ = lax.scan(accumulate, start_total, (blocks, masks))
    return (total * (1.0 / math.sqrt(NAUX * NOCC))).astype(jnp.bfloat16)
```

```python
import functools
import math

import jax
import jax.numpy as jnp
from jax import lax
from jax.experimental import pallas as pl
from jax.experimental.pallas import tpu as pltpu
from jax.sharding import PartitionSpec as P

BLOCK = 128
LANES = 128


def scoped(name):
    def wrap(call):
        return call
    return wrap


ZINT = 5.66
OWN = (2.0, 9.7, 26.5)
DOTS = (8.0, 16.6, 40.3)
PACE = (0.8, 1.0, 1.4)
HALF = (16.5, 28.4, 54.4)
LINE = (19.3, 35.8, 60.7)
FIRST = (3.9, 7.5, 0.5)
HOP = (8.9, 7.2, 4.9)
LAST = (8.0, 1.0, 2.4)
WIDE = 1.4


def place(groups, i):
    hop, sub = (i + 2) // 4, (i + 2) % 4
    middle = 2 * hop // groups
    edge = 1 - (hop + groups - 1) // groups + middle
    side = (1 - middle) * (sub % 2)
    other = edge * (sub % 2) + (1 - edge) * (sub // 2)
    return hop + side * (groups - 2 * hop), other


def plan(groups, aux, pieces, stages, tiles, early):
    chunks, bas = len(pieces), 2 * groups
    timed = []

    def at(time, *op):
        timed.append((time, len(timed), op))

    def when(table, j):
        return table[min(j, len(table) - 1)] + max(0, j - len(table) + 1) * 3 * ZINT

    for j in range(chunks):
        if j > 0:
            at(when(OWN, j), "own", j)
        for i in range(bas):
            offset, other = place(groups, i)
            offset = offset % groups
            hop = min(offset, groups - offset)
            time = when(DOTS, j) + PACE[min(j, 2)] * i * 8 / bas
            if other == 0 and offset == hop > 0:
                at(time - 0.003 - 100 * (j == 0 and hop == 1), "take", j, hop, 0)
                if 2 * hop < groups:
                    at(time - 0.002, "take", j, hop, 1)
            if other == 1:
                at(time - 0.001, "pair", j, offset)
            if j == 0 and i == early:
                at(-50, "late")
            if j == 0 and i >= early:
                at(time - 0.0005, "mask", i)
            at(time, "dot", j, i)
        at(when(HALF, j), "half", j)
        k = min(j, 2)
        for d in range(aux):
            for q in range(pieces[j]):
                if d == 0:
                    time = when(HALF, j) + 0.001
                    begin = time + FIRST[k] + q // 2 * ZINT / pieces[j] * WIDE
                    end = time + FIRST[k] + 3 * HOP[k] + LAST[k]
                else:
                    time = when(LINE, j) + ZINT * (d - 1 + q / pieces[j])
                    begin = time + FIRST[k]
                    end = begin + 2 * HOP[k] + LAST[k]
                at(time, "line", j, d, q)
                for s in range(stages):
                    at(begin + HOP[k] * s + 0.0001, "stage", j, d, q, s)
                at(end + 0.0001, "close", j, d, q)
    times = {op: time for time, _, op in timed}
    needs = []
    for j in range(chunks):
        if j > 0:
            needs += [(("own", j), ("take", j, 1, 0)), (("own", j), ("dot", j, 0)), (("half", j - 1), ("dot", j, 0)),
                      (("take", j - 1, 1, 0), ("own", j))]
        for hop in range(1, groups // 2 + 1):
            needs += [(("take", j, hop, 0), ("take", j, hop, 1)), (("take", j, hop, 0), ("take", j, hop + 1, 0)),
                      (("take", j, hop, 1), ("take", j, hop + 1, 0))]
        for i in range(bas):
            offset, other = place(groups, i)
            offset = offset % groups
            hop = min(offset, groups - offset)
            needs += [(("take", j, hop, 0), ("dot", j, i)), (("take", j, hop, 1), ("dot", j, i))]
            if other == 1:
                needs.append((("pair", j, offset), ("dot", j, i)))
                needs += [(("take", j, hop, 0), ("pair", j, offset)), (("take", j, hop, 1), ("pair", j, offset))]
            if j == 0:
                needs += [(("mask", i), ("dot", 0, i)), (("late",), ("mask", i))]
            needs.append((("dot", j, i), ("dot", j, i + 1) if i + 1 < bas else ("half", j)))
        for q in range(pieces[j - 1] if j > 0 else 0):
            needs += [(("close", j - 1, d, q), ("close", j, aux - 1, 0)) for d in range(aux)]
        for q in range(pieces[j]):
            if j == chunks - 1 and aux > 1:
                needs += [(("line", j, d, q), ("close", j, aux - 1, 0)) for d in range(aux)]
                needs += [(("close", j, d, q), ("close", j, aux - 1, q)) for d in range(aux - 1)]
            needs.append((("half", j), ("line", j, 0, q)))
            for d in range(1, aux):
                needs += [(("line", j, 0, own), ("line", j, d, q)) for own in range(pieces[j])]
    needs = [(first, then) for first, then in needs if first in times and then in times]
    moved = True
    while moved:
        moved = False
        for first, then in needs:
            if times[first] > times[then] - 0.00001:
                times[first] = times[then] - 0.00002
                moved = True
    order = sorted(times, key=lambda op: times[op])

    steps, waiting, closed = [], [], [0] * chunks
    for op in order:
        steps.append(op)
        if op[0] == "close":
            j, d, q = op[1:]
            closed[j] += 1
            if closed[j] == aux * pieces[j] and j < chunks - 1:
                waiting += [("exchange", j, low, min(tiles, low + 2)) for low in range(0, tiles, 2)]
            if j == chunks - 1 and d == aux - 1:
                if q == 0:
                    steps[-1:] = waiting + steps[-1:]
                    waiting = []
                steps.append(("final", q))
        if op[0] == "line" and waiting:
            steps.append(waiting.pop(0))
    return steps


def kernel(groups, aux, scale, integrals, screen, coefs, weights, out,
           ints, fac, acc, right, left, wt, total, result, keep,
           load_sem, ring_send, ring_recv, pair_send, pair_recv,
           line_recv, up_send, down_send,
           lring_send, lring_recv, lpair_send, lpair_recv, lown_sem, out_sem):
    rows, basis = integrals.shape[1:]
    chunks = fac.shape[0]
    half_rows = rows // 2
    spread = left.shape[1]
    sets = spread // 2
    row_blocks = rows // BLOCK
    bas = 2 * groups
    bas_me = lax.axis_index("bas")
    z = lax.axis_index("aux")
    core = bas_me % 2
    half_ring = groups // 2
    last = chunks - 1

    def swap(index):
        upper = index // half_ring
        return index + upper * (3 * half_ring - 1 - 2 * index)

    pos = swap(bas_me // 2)

    def device_at(position, which):
        return 2 * swap(position % groups) + which

    partner = bas_me - core + (1 - core)

    def ring_to(side):
        return device_at(pos + groups + 1 - 2 * side, core)

    def origin(offset, which):
        return device_at(pos + groups - offset, which)

    def remote(src, dst, send, recv, bas=None, aux_to=None):
        return pltpu.make_async_remote_copy(
            src_ref=src, dst_ref=dst, send_sem=send, recv_sem=recv,
            device_id={"bas": bas_me if bas is None else bas, "aux": z if aux_to is None else aux_to},
            device_id_type=pl.DeviceIdType.MESH)

    finish = {}

    def guard(condition, action):
        pl.when(condition)(lambda: action())

    def device_of(i):
        offset, other = place(groups, i)
        return device_at(pos + groups - offset, (core + other) % 2)

    def int_load(i):
        device = device_of(i)
        cols = pl.ds(pl.multiple_of(device * rows, LANES), rows)
        return pltpu.make_async_copy(integrals.at[0, :, cols], ints.at[device, :, pl.ds(0, rows)], load_sem.at[chunks + i])

    def fac_load(j):
        return pltpu.make_async_copy(coefs.at[:, pl.ds(j * LANES, LANES)], fac.at[j, bas_me], load_sem.at[j])

    for j in range(chunks):
        fac_load(j).start()

    early = bas // 2
    for i in range(early):
        int_load(i).start()

    barrier = pltpu.get_barrier_semaphore()
    for other in (ring_to(0), ring_to(1), partner):
        pl.semaphore_signal(barrier, inc=1, device_id={"bas": other, "aux": z}, device_id_type=pl.DeviceIdType.MESH)

    @pl.when(z > 0)
    def _():
        pl.semaphore_signal(barrier, inc=1, device_id={"bas": bas_me, "aux": z - 1}, device_id_type=pl.DeviceIdType.MESH)

    @pl.when(z < aux - 1)
    def _():
        pl.semaphore_signal(barrier, inc=1, device_id={"bas": bas_me, "aux": z + 1}, device_id_type=pl.DeviceIdType.MESH)

    peers = 3 + (z + aux - 1) // aux + (2 * aux - 2 - z) // aux

    @scoped("expand")
    def expand():
        flags = screen[0].astype(jnp.float32)
        wide = jnp.concatenate(
            [jnp.broadcast_to(flags[r:r + 1], (16, flags.shape[1])) for r in range(row_blocks)], axis=0)
        wide = wide.astype(jnp.bfloat16)
        span = basis // 8

        def body(q, carry):
            block = (lax.broadcasted_iota(jnp.int32, (flags.shape[1], span), 1) // BLOCK) + q * (span // BLOCK)
            here = block == lax.broadcasted_iota(jnp.int32, (flags.shape[1], span), 0)
            pick = jnp.where(here, 1.0, 0.0).astype(jnp.bfloat16)
            values = jnp.dot(wide, pick, preferred_element_type=jnp.float32)
            keep[:, pl.ds(pl.multiple_of(q * span, LANES), span)] = values.astype(jnp.bfloat16)
            return carry

        lax.fori_loop(0, 8, body, 0)

    @scoped("barrier")
    def enter():
        pl.semaphore_wait(barrier, peers)

    enter()

    def fac_piece(j, offset, half, which):
        return fac.at[j, origin(offset, which), pl.ds(half * half_rows, half_rows)]

    def reaches(hop, side):
        if 2 * hop < groups:
            return (side, 1 - side)
        return (side,) if 2 * hop == groups else ()

    def shift(hop, side):
        return hop if side == 0 else (groups - hop) % groups

    def ring_copy(j, side, hop, half):
        piece = fac_piece(j, shift(hop - 1, side), half, core)
        at = (j, side, hop - 1, half)
        return remote(piece, piece, ring_send.at[at], ring_recv.at[at], bas=ring_to(side))

    def ring_arrival(j, side, hop, half):
        piece = fac_piece(j, shift(hop, side), half, core)
        at = (j, side, hop - 1, half)
        return remote(piece, piece, ring_send.at[at], ring_recv.at[at], bas=ring_to(side))

    def pair_copy(j, offset, half, which):
        piece = fac_piece(j, offset, half, which)
        at = (j, offset, half)
        return remote(piece, piece, pair_send.at[at], pair_recv.at[at], bas=partner)

    def send_ring(j, side, hop, half):
        ring_copy(j, side, hop, half).start()
        finish["ring", j, side, hop, half] = lambda: ring_copy(j, side, hop, half).wait_send()

    def send_pair(j, offset, half):
        pair_copy(j, offset, half, core).start()
        finish["pair", j, offset, half] = lambda: pair_copy(j, offset, half, core).wait_send()

    @scoped("ring_own")
    def ring_own(j):
        fac_load(j).wait()
        for turn in (0, 1):
            for side in (0, 1):
                if turn < len(reaches(1, side)):
                    send_ring(j, side, 1, reaches(1, side)[turn])
        for half in (0, 1):
            send_pair(j, 0, half)

    @scoped("ring_take")
    def ring_take(j, hop, turn):
        for side in (0, 1):
            if turn < len(reaches(hop, side)):
                half = reaches(hop, side)[turn]
                ring_arrival(j, side, hop, half).wait_recv()
                if half in reaches(hop + 1, side):
                    send_ring(j, side, hop + 1, half)
                send_pair(j, shift(hop, side), half)

    def pair_wait(j, offset):
        for half in (0, 1):
            pair_copy(j, offset, half, 1 - core).wait_recv()

    @scoped("mask")
    def mask(i):
        int_load(i).wait()
        device = device_of(i)
        first = device * (rows // BLOCK)

        def body(q, carry):
            flags = pl.ds(pl.multiple_of((first + q) * BLOCK, BLOCK), BLOCK)
            cols = pl.ds(pl.multiple_of(q * BLOCK, BLOCK), BLOCK)
            for r in range(row_blocks):
                flag = keep[pl.ds(r * 16, 16), flags]
                for a in range(BLOCK // 16):
                    at = pl.ds(r * BLOCK + a * 16, 16)
                    ints[device, at, cols] = ints[device, at, cols] * flag
            return carry

        lax.fori_loop(0, rows // BLOCK, body, 0, unroll=2)

    pieces = [2] * last + [4]

    def span_of(j, q):
        return pl.ds(q * (rows // pieces[j]), rows // pieces[j])

    def member(d, side):
        if side == 0:
            return z - d, z >= d
        return z + d, z + d < aux

    def sides(d):
        return (0,) if d == 0 else (0, 1)

    def weigh(j, p, q):
        values = right[j, p, span_of(j, q)].astype(jnp.float32) * weights[:, pl.ds(j * LANES, LANES)]
        wt[j, pl.ds(pl.multiple_of(p * LANES, LANES), LANES), span_of(j, q)] = values.T.astype(jnp.bfloat16)

    def line_piece(j, p, q):
        return right.at[j, p, span_of(j, q)]

    def line_copy(j, p, q, to):
        piece = line_piece(j, p, q)
        sem = (down_send, up_send)[to]
        return remote(piece, piece, sem.at[j, p, q], line_recv.at[j, p, q], aux_to=z - 1 + 2 * to)

    def line_send(j, d, side, q, to):
        def on(action):
            p, there = member(d, side)
            room = (z < aux - 1) if to else (z > 0)
            guard(there & room, lambda: action(line_copy(j, p, q, to)))

        on(lambda copy: copy.start())
        finish["line", j, d, side, q, to] = lambda: on(lambda copy: copy.wait_send())

    def left_piece(j, s, p, q):
        return left.at[j, s, p, span_of(j, q)]

    def lring_copy(src, j, t, p, q):
        at = (j, t, p, q)
        return remote(src, left_piece(j, 2 * t + core, p, q), lring_send.at[at], lring_recv.at[at], bas=ring_to(q % 2))

    def lpair_copy(src, j, t, p, q):
        at = (j, t, p, q)
        return remote(src, left_piece(j, 2 * t + core, p, q), lpair_send.at[at], lpair_recv.at[at], bas=partner)

    def lown_copy(j, t, p, q):
        return pltpu.make_async_copy(line_piece(j, p, q), left_piece(j, 2 * t + core, p, q), lown_sem.at[j, t, p, q])

    def away(t):
        return (pos - swap(z * sets + t) + groups) % groups

    def left_start(j, d, side, q):
        for t in range(sets):
            def on(action, t=t):
                p, there = member(d, side)
                guard(there & (away(t) == 0), lambda: action(line_piece(j, p, q), j, t, p, q))

            def go(src, j, t, p, q):
                lring_copy(src, j, t, p, q).start()
                lpair_copy(src, j, t, p, q).start()
                lown_copy(j, t, p, q).start()

            def end(src, j, t, p, q):
                lring_copy(src, j, t, p, q).wait_send()
                lpair_copy(src, j, t, p, q).wait_send()

            on(go)
            finish["left", j, d, side, q, t] = lambda on=on, end=end: on(end)

    stages = min(3, groups - 1)

    def left_stage(j, d, side, q, stage):
        for t in range(sets):
            def on(action, onward, t=t):
                p, there = member(d, side)
                distance = away(t)
                hops = distance if q % 2 == 0 else groups - distance
                takes = there & (distance != 0) & ((stages * (hops - 1)) // max(1, groups - 1) == stage)
                if onward:
                    takes = takes & (hops < groups - 1)
                guard(takes, lambda: action(left_piece(j, 2 * t + core, p, q), j, t, p, q))

            on(lambda *a: lring_copy(*a).wait_recv(), False)
            on(lambda *a: lring_copy(*a).start(), True)
            on(lambda *a: lpair_copy(*a).start(), False)

            def end(on=on):
                on(lambda *a: lpair_copy(*a).wait_send(), False)
                on(lambda *a: lring_copy(*a).wait_send(), True)

            finish["stage", j, d, side, q, stage, t] = end

    def left_close(j, d, side, q):
        p, there = member(d, side)
        for t in range(sets):
            guard(there & (away(t) == 0), lambda t=t: lown_copy(j, t, p, q).wait())

            def from_partner(t=t):
                dst = left_piece(j, 2 * t + 1 - core, p, q)
                at = (j, t, p, q)
                remote(dst, dst, lpair_send.at[at], lpair_recv.at[at], bas=partner).wait_recv()

            guard(there, from_partner)

    @scoped("line")
    def line_event(j, d, q):
        for side in sides(d):
            if d == 0:
                line_send(j, d, side, q, 1)
                line_send(j, d, side, q, 0)
            else:
                p, there = member(d, side)
                guard(there, lambda p=p: line_copy(j, p, q, 1).wait_recv())
                line_send(j, d, side, q, 1 - side)
        for side in sides(d):
            left_start(j, d, side, q)
        for side in sides(d):
            p, there = member(d, side)
            guard(there, lambda p=p: weigh(j, p, q))

    tile_n = min(256, rows // 4)
    tiles_in = rows // tile_n
    tiles = spread * tiles_in

    def out_copy(i):
        at = pl.ds(i * tile_n, tile_n)
        return pltpu.make_async_copy(result.at[at], out.at[at], out_sem.at[i])

    def tile(j, s, r):
        at = pl.ds(pl.multiple_of(r * tile_n, tile_n), tile_n)
        lhs = jnp.concatenate([left[j, s, p, at, :] for p in range(aux)], axis=1)
        to = pl.ds(pl.multiple_of((s * tiles_in + r) * tile_n, tile_n), tile_n)
        if j > 0:
            part = total[to, :] + jnp.dot(lhs, wt[j], preferred_element_type=jnp.float32)
        else:
            part = jnp.dot(lhs, wt[j], preferred_element_type=jnp.float32)
        if j == last:
            result[to, :] = (part * scale).astype(jnp.bfloat16)
        else:
            total[to, :] = part

    @scoped("exchange")
    def exchange(j, low, high):
        def body(i, carry):
            tile(j, i // tiles_in, i % tiles_in)
            return carry

        lax.fori_loop(low, high, body, 0)

    @scoped("final")
    def final(q):
        per = tiles_in // pieces[last]

        def body(i, carry):
            tile(last, i // per, q * per + i % per)
            return carry

        lax.fori_loop(0, spread * per, body, 0)
        for s in range(spread):
            for r in range(q * per, q * per + per):
                out_copy(s * tiles_in + r).start()

    @scoped("late")
    def late():
        for i in range(early, bas):
            int_load(i).start()

    @scoped("half")
    def close_half(j):
        right[j, z] = acc[j].astype(jnp.bfloat16)

    def stage(j, d, q, s):
        for side in sides(d):
            left_stage(j, d, side, q, s)

    def close(j, d, q):
        for side in sides(d):
            left_close(j, d, side, q)

    kinds = {"own": ring_own, "take": ring_take, "pair": pair_wait, "late": late, "mask": mask, "half": close_half,
             "line": line_event, "stage": stage, "close": close, "exchange": exchange, "final": final}

    def do(op):
        kinds[op[0]](*op[1:])

    steps = plan(groups, aux, pieces, stages, tiles, early)

    def chunk(j, ops):
        todo = {i: [] for i in range(bas)}
        i = 0
        for op in ops:
            if op[0] == "dot":
                i += 1
            else:
                todo[i].append(op)

        def body(i, carry):
            @pl.when(i == 0)
            def _():
                acc[j] = jnp.zeros(acc.shape[1:], acc.dtype)

            for k in range(bas):
                if todo[k]:
                    @pl.when(i == k)
                    def _(k=k):
                        for op in todo[k]:
                            do(op)

            device = device_of(i)
            acc[j] = acc[j] + jnp.dot(ints[device, :, pl.ds(0, rows)], fac[j, device], preferred_element_type=jnp.float32)
            return carry

        lax.fori_loop(0, bas, body, 0)

    ring_own(0)
    expand()
    for i in range(early):
        mask(i)
    n = 0
    while n < len(steps):
        op = steps[n]
        if op[0] == "dot":
            end = steps.index(("dot", op[1], bas - 1))
            chunk(op[1], steps[n:end + 1])
            n = end + 1
        else:
            do(op)
            n += 1
    for action in finish.values():
        action()
    for n in range(tiles):
        out_copy(n).wait()


def shards(integrals, screen, coefficients, weights):
    _, rows, basis = integrals.shape
    occ = coefficients.shape[1]
    bas, aux = lax.axis_size("bas"), lax.axis_size("aux")
    groups, spread, chunks = bas // 2, bas // aux, occ // LANES
    sets = spread // 2
    tiles = spread * rows // min(256, rows // 4)
    reach = max(1, groups // 2)
    scale = 1.0 / math.sqrt(integrals.shape[0] * aux * occ)
    dma = pltpu.SemaphoreType.DMA
    bf16, f32 = jnp.bfloat16, jnp.float32
    return pl.pallas_call(
        functools.partial(kernel, groups, aux, scale),
        out_shape=jax.ShapeDtypeStruct((spread * rows, rows), bf16),
        in_specs=[
            pl.BlockSpec(memory_space=pl.ANY),
            pl.BlockSpec(memory_space=pltpu.VMEM),
            pl.BlockSpec(memory_space=pl.ANY),
            pl.BlockSpec(memory_space=pltpu.VMEM),
        ],
        out_specs=pl.BlockSpec(memory_space=pl.ANY),
        scratch_shapes=[
            pltpu.VMEM((bas, rows, rows + LANES), bf16),
            pltpu.VMEM((chunks, bas, rows, LANES), bf16),
            pltpu.VMEM((chunks, rows, LANES), f32),
            pltpu.VMEM((chunks, aux, rows, LANES), bf16),
            pltpu.VMEM((chunks, spread, aux, rows, LANES), bf16),
            pltpu.VMEM((chunks, aux * LANES, rows), bf16),
            pltpu.VMEM((spread * rows, rows), f32),
            pltpu.VMEM((spread * rows, rows), bf16),
            pltpu.VMEM((rows // BLOCK * 16, basis), bf16),
            dma((chunks + bas,)),
            dma((chunks, 2, reach, 2)), dma((chunks, 2, reach, 2)),
            dma((chunks, groups, 2)), dma((chunks, groups, 2)),
            dma((chunks, aux, 4)), dma((chunks, aux, 4)), dma((chunks, aux, 4)),
            dma((chunks, sets, aux, 4)), dma((chunks, sets, aux, 4)),
            dma((chunks, sets, aux, 4)), dma((chunks, sets, aux, 4)),
            dma((chunks, sets, aux, 4)),
            dma((tiles,)),
        ],
        compiler_params=pltpu.CompilerParams(
            collective_id=0, has_side_effects=True, vmem_limit_bytes=62 * 1024 * 1024),
    )(integrals, screen, coefficients, weights.reshape(1, occ))


def solution(mesh):
    in_specs = (P("aux", "bas", None), P("aux", "bas", None), P("bas", None), P())
    out_specs = P("aux", "bas")
    return jax.shard_map(shards, mesh=mesh, in_specs=in_specs, out_specs=out_specs, check_vma=False)
```
